32 devices in a mesh: dp: 8 (over y, x, core), tensor: 4 (over z).
Axes of the slice: x: 2, y: 2, z: 4, core: 2. Of those that a mesh axis runs over, the one named last changes fastest.
Arguments:
- hidden: bfloat16 [8192, 1536], P('dp'), may hold values from -6 to 6
- norm_gain: float32 [1536], replicated, may hold values from 0.25 to 1.75
- zx_proj: bfloat16 [1536, 2, 3072], P(None, None, 'tensor'), may hold values from -0.15625 to 0.15625
- bc_proj: bfloat16 [1536, 256], replicated, may hold values from -0.15625 to 0.15625
- dt_proj: bfloat16 [1536, 48], P(None, 'tensor'), may hold values from -0.15625 to 0.15625
- conv_x: float32 [5, 3072], P(None, 'tensor'), may hold values from -3 to 3
- conv_bc: float32 [5, 256], replicated, may hold values from -3 to 3
- dt_bias: float32 [48], P('tensor'), may hold values from -7 to -3
- a_log: float32 [48], P('tensor'), may hold values from -4 to 0.5
- d_skip: float32 [48], P('tensor'), may hold values from 0.5 to 1.5
- gate_gain: float32 [3072], P('tensor'), may hold values from 0.25 to 1.75
- out_proj: bfloat16 [1536, 3072], P(None, 'tensor'), may hold values from -0.109375 to 0.109375
- cotangent: bfloat16 [8192, 1536], P('dp'), may hold values from -6 to 6
Outputs:
- block_out: bfloat16 [8192, 1536], P('dp')
- grad_hidden: bfloat16 [8192, 1536], P('dp')
- grad_norm_gain: float32 [1536], replicated
- grad_zx_proj: float32 [1536, 2, 3072], P('dp', None, 'tensor')
- grad_bc_proj: float32 [1536, 256], P('dp')
- grad_dt_proj: float32 [1536, 48], P('dp', 'tensor')
- grad_conv_x: float32 [5, 3072], P(None, 'tensor')
- grad_conv_bc: float32 [5, 256], replicated
- grad_dt_bias: float32 [48], P('tensor')
- grad_a_log: float32 [48], P('tensor')
- grad_d_skip: float32 [48], P('tensor')
- grad_gate_gain: float32 [3072], P('tensor')
- grad_out_proj: float32 [1536, 3072], P('dp', 'tensor')
The draws below stay inside these ranges and needn't reach their ends.
All inputs are finite; a program needn't handle non-finite values.
Results may differ from the reference program's by a relative error of at most 0.005.
The reference program's roundings to bfloat16 on the way count: a program that leaves them out, or rounds other values in their place, can miss the bound.
Values may be sent and summed in bfloat16 or wider, within the bound.
No kernel may reach another device: no remote copies, remote signals or barrier semaphores. Data moves between devices by JAX's collectives and lax.ppermute only.
A program may use at most 192 MiB of HBM per device.

```python
import jax
import jax.numpy as jnp
from jax import lax

D = 1536
HEADS = 48
HEADDIM = 64
STATE = 128
KCONV = 4
BLOCK_LEN = 256
INNER = 3072
LENGTH = 8192
SEQS = 1
TOKENS = 8192


def level_of(own_key, shape, cuts, low, top_value):
    def one(position, blocks):
        heights = jax.random.uniform(jax.random.fold_in(jax.random.fold_in(own_key, 6), position), (blocks,), jnp.float32, low / len(cuts), top_value / len(cuts))
        return jnp.repeat(jnp.exp(heights), shape[position] // blocks).reshape((-1,) + (1,) * (len(shape) - position - 1))

    level = one(*cuts[0])
    for cut in cuts[1:]:
        level = level * one(*cut)
    return level


def gaussian(own_key, shape, scale, reach, split=(), held_as=jnp.bfloat16):
    values = jax.random.normal(own_key, shape, jnp.float32) * scale
    if len(split) > 0:
        values = level_of(own_key, shape, split, -0.22, 0.18) * values
    return jnp.clip(values, min=-reach, max=reach).astype(held_as)


def setup_inputs(seed: int = 0) -> dict:
    splits = jax.random.split(jax.random.key(seed), 14)
    hidden = gaussian(splits[0], (TOKENS, D), 1.0, 6.0, ((0, 8),))
    norm_gain = jnp.clip(1.0 + 0.15 * jax.random.normal(splits[1], (D,), jnp.float32), 0.25, 1.75)
    zx_proj = gaussian(splits[2], (D, 2, INNER), D ** -0.5, 0.15625, ((2, 4),))
    bc_proj = gaussian(splits[3], (D, 2 * STATE), D ** -0.5, 0.15625)
    dt_proj = gaussian(splits[4], (D, HEADS), D ** -0.5, 0.15625, ((1, 4),))
    conv_x = gaussian(splits[5], (KCONV + 1, INNER), KCONV ** -0.5, 3.0, ((1, 4),), jnp.float32)
    conv_bc = gaussian(splits[6], (KCONV + 1, 2 * STATE), KCONV ** -0.5, 3.0, (), jnp.float32)
    dt_bias = jnp.clip(-7.0 + 4.0 * jax.random.uniform(splits[7], (HEADS,), jnp.float32) ** level_of(splits[7], (HEADS,), ((0, 4),), -0.2, 0.2), -7.0, -3.0)
    a_log = jnp.clip(-4.0 + 4.5 * jax.random.uniform(splits[8], (HEADS,), jnp.float32) ** level_of(splits[8], (HEADS,), ((0, 4),), -0.2, 0.2), -4.0, 0.5)
    d_skip = jnp.clip(0.5 + 1.0 * jax.random.uniform(splits[9], (HEADS,), jnp.float32) ** level_of(splits[9], (HEADS,), ((0, 4),), -0.2, 0.2), 0.5, 1.5)
    gate_gain = jnp.clip(1.0 + 0.15 * jax.random.normal(splits[10], (INNER,), jnp.float32), 0.25, 1.75)
    out_proj = gaussian(splits[11], (D, INNER), INNER ** -0.5, 0.109375, ((1, 4),))
    cotangent = gaussian(splits[12], (TOKENS, D), 1.0, 6.0, ((0, 8),))
    return dict(hidden=hidden, norm_gain=norm_gain, zx_proj=zx_proj, bc_proj=bc_proj, dt_proj=dt_proj, conv_x=conv_x, conv_bc=conv_bc, dt_bias=dt_bias, a_log=a_log, d_skip=d_skip, gate_gain=gate_gain, out_proj=out_proj, cotangent=cotangent)


EPSILON = 1e-05
PRECISE = lax.Precision.HIGHEST

@jax.custom_vjp
def low(v):
    return lax.optimization_barrier(v.astype(jnp.bfloat16)).astype(jnp.float32)

@jax.custom_vjp
def low_back(v):
    return v

def low_keep(v):
    return (low(v), None)

def low_pass(kept, grad):
    return (grad,)

def back_keep(v):
    return (v, None)

def back_low(kept, grad):
    return (low(grad),)
low.defvjp(low_keep, low_pass)
low_back.defvjp(back_keep, back_low)

def swish_value(operand):
    return operand * jax.nn.sigmoid(operand)

def causal_conv(signal, weights):
    length = signal.shape[0]
    padded = jnp.pad(signal, ((KCONV - 1, 0), (0, 0)))
    result = weights[KCONV] + weights[0] * padded[0:length]
    for tap_index in range(1, KCONV):
        result = result + weights[tap_index] * padded[tap_index:tap_index + length]
    return result

def block_step(carried, pieces):
    inputs, b_rows, c_rows, step_size, log_decay = pieces
    length = step_size.shape[0]
    cumulative = jnp.cumsum(log_decay, axis=0)
    row_index = lax.broadcasted_iota(jnp.int32, (length, length), 0)
    col_index = lax.broadcasted_iota(jnp.int32, (length, length), 1)
    within = (row_index >= col_index)[:, :, None]
    spread = cumulative[:, None, :] - cumulative[None, :, :]
    decay_pairs = jnp.where(within, jnp.exp(jnp.where(within, spread, 0.0)), 0.0)
    affinity = jnp.dot(c_rows, b_rows.T, precision=PRECISE)
    mixing = affinity[:, :, None] * decay_pairs * step_size[None, :, :]
    intra_out = jnp.einsum('ijh,jhp->ihp', mixing, inputs, precision=PRECISE)
    inter_out = jnp.exp(cumulative)[:, :, None] * jnp.einsum('in,hpn->ihp', c_rows, carried, precision=PRECISE)
    to_end = jnp.exp(cumulative[-1][None, :] - cumulative) * step_size
    sent_state = jnp.einsum('jhp,jn->hpn', to_end[:, :, None] * inputs, b_rows, precision=PRECISE)
    next_state = jnp.exp(cumulative[-1])[:, None, None] * carried + sent_state
    return (next_state, intra_out + inter_out)

def ssd_scan(inputs, b_rows, c_rows, step_size, log_decay):
    length = inputs.shape[0]
    block_count = length // BLOCK_LEN
    pieces = (inputs.reshape(block_count, BLOCK_LEN, HEADS, HEADDIM), b_rows.reshape(block_count, BLOCK_LEN, STATE), c_rows.reshape(block_count, BLOCK_LEN, STATE), step_size.reshape(block_count, BLOCK_LEN, HEADS), log_decay.reshape(block_count, BLOCK_LEN, HEADS))
    start_state = jnp.zeros((HEADS, HEADDIM, STATE), jnp.float32)
    final_state, outputs = lax.scan(jax.checkpoint(block_step), start_state, pieces)
    return outputs.reshape(length, HEADS, HEADDIM)

def mixer(residual, norm_gain, zx_proj, bc_proj, dt_proj, conv_x, conv_bc, dt_bias, a_log, d_skip, gate_gain, out_proj):
    length = residual.shape[0]
    normed = residual * lax.rsqrt(lax.optimization_barrier(jnp.mean(residual * residual, axis=1, keepdims=True)) + EPSILON)
    normed_low = low(normed * norm_gain)
    zx_out = jnp.einsum('td,dki->tki', normed_low, zx_proj, precision=PRECISE)
    gate_in = low_back(low(zx_out[:, 0]))
    inner_in = low_back(low(zx_out[:, 1]))
    bc_in = low_back(low(jnp.dot(normed_low, bc_proj, precision=PRECISE)))
    dt_raw = low_back(jnp.dot(normed_low, dt_proj, precision=PRECISE))
    inputs = swish_value(causal_conv(inner_in, conv_x)).reshape(length, HEADS, HEADDIM)
    bc_act = swish_value(causal_conv(bc_in, conv_bc))
    step_size = jax.nn.softplus(dt_raw + dt_bias)
    log_decay = -jnp.exp(a_log) * step_size
    ssd_out = ssd_scan(inputs, bc_act[:, :STATE], bc_act[:, STATE:], step_size, log_decay)
    ssd_out = ssd_out + d_skip[:, None] * inputs
    gated_out = ssd_out.reshape(length, INNER) * swish_value(gate_in)
    square_mean = lax.optimization_barrier(jnp.mean(gated_out * gated_out, axis=1, keepdims=True))
    gated_low = low(gated_out * gate_gain)
    branch_proj = low_back(jnp.dot(gated_low, out_proj.T, precision=PRECISE))
    return residual + lax.rsqrt(square_mean + EPSILON) * branch_proj

def reference(hidden, norm_gain, zx_proj, bc_proj, dt_proj, conv_x, conv_bc, dt_bias, a_log, d_skip, gate_gain, out_proj, cotangent):
    params = tuple((param_value.astype(jnp.float32) for param_value in (norm_gain, zx_proj, bc_proj, dt_proj, conv_x, conv_bc, dt_bias, a_log, d_skip, gate_gain, out_proj)))
    seq_hidden = hidden.astype(jnp.float32).reshape(SEQS, LENGTH, D)
    seq_cot = cotangent.astype(jnp.float32).reshape(SEQS, LENGTH, D)

    def sequence_pass(totals, sequence_pair):
        seq_out, pullback = jax.vjp(mixer, sequence_pair[0], *params)
        grads = pullback(sequence_pair[1])
        totals = tuple((total_item + grad_item for total_item, grad_item in zip(totals, grads[1:])))
        return (totals, (seq_out.astype(jnp.bfloat16), grads[0].astype(jnp.bfloat16)))
    zero_grads = tuple((jnp.zeros_like(param_value) for param_value in params))
    totals, (seq_outs, seq_grads) = lax.scan(sequence_pass, zero_grads, (seq_hidden, seq_cot))
    return (seq_outs.reshape(TOKENS, D), seq_grads.reshape(TOKENS, D), totals[0], totals[1], totals[2], totals[3], totals[4], totals[5], totals[6], totals[7], totals[8], totals[9], totals[10])
```

```python
import jax
import jax.numpy as jnp
from jax import lax
from jax.sharding import PartitionSpec as P

KCONV = 4
BLOCK_LEN = 256
SEQ_DEVS = 8


EPSILON = 1e-05
PRECISE = lax.Precision.HIGHEST


def shifted(x, axis, by):
    length = lax.axis_size(axis)
    pairs = [(i, i + by) for i in range(length) if 0 <= i + by < length]
    return lax.ppermute(x, axis, pairs)


def exchange(x, axis, bit):
    length = lax.axis_size(axis)
    return lax.ppermute(x, axis, [(i, i ^ bit) for i in range(length)])


def entering(own, decay, axis, reverse):
    position = lax.axis_index(axis) % SEQ_DEVS
    shape = own.shape
    wide = (decay.shape[0],) + (1,) * (len(shape) - 1)
    before = jnp.zeros_like(own)
    before_decay = jnp.ones_like(decay)
    total = own
    total_decay = decay
    bit = 1
    while bit < SEQ_DEVS:
        other = exchange(total, axis, bit)
        other_decay = exchange(total_decay, axis, bit)
        later = (position & bit) != 0
        if reverse:
            later = jnp.logical_not(later)
        before = jnp.where(later, before + before_decay.reshape(wide) * other, before)
        before_decay = jnp.where(later, before_decay * other_decay, before_decay)
        total = jnp.where(
            later,
            total + total_decay.reshape(wide) * other,
            other + other_decay.reshape(wide) * total,
        )
        total_decay = total_decay * other_decay
        bit = bit * 2
    return before


def fold(pieces, axis, bit, mine):
    sent = lax.dynamic_index_in_dim(pieces, 1 - mine, 0, keepdims=False)
    kept = lax.dynamic_index_in_dim(pieces, mine, 0, keepdims=False)
    return kept + exchange(sent.astype(jnp.bfloat16), axis, bit).astype(jnp.float32)


def halving_sum(local, axis):
    length = lax.axis_size(axis)
    index = lax.axis_index(axis)
    rows, width = local.shape
    kept = local.reshape(length, rows // length, width)
    bit = 1
    while bit < length:
        count = kept.shape[0] // 2
        pieces = jnp.swapaxes(kept.reshape((count, 2) + kept.shape[1:]), 0, 1)
        kept = fold(pieces, axis, bit, (index // bit) % 2)
        bit = bit * 2
    return kept[0]


def swish_value(operand):
    return operand * jax.nn.sigmoid(operand)


def swish_slope(operand):
    logistic = jax.nn.sigmoid(operand)
    return logistic * (1.0 + operand * (1.0 - logistic))


def product_nt(first_op, second_op):
    return lax.dot_general(
        first_op, second_op, (((1,), (1,)), ((), ())), preferred_element_type=jnp.float32
    )


def product_tn(first_op, second_op):
    return lax.dot_general(
        first_op, second_op, (((0,), (0,)), ((), ())), preferred_element_type=jnp.float32
    )


def shards(
    hidden,
    norm_gain,
    zx_proj,
    bc_proj,
    dt_proj,
    conv_x,
    conv_bc,
    dt_bias,
    a_log,
    d_skip,
    gate_gain,
    out_proj,
    cotangent,
):
    tokens = hidden.shape[0]
    model_width = hidden.shape[1]
    inner_local = zx_proj.shape[2]
    heads_local = dt_proj.shape[1]
    head_size = inner_local // heads_local
    state_size = bc_proj.shape[1] // 2
    inner_total = inner_local * lax.axis_size("tensor")
    blocks = tokens // BLOCK_LEN
    position = lax.axis_index("dp") % SEQ_DEVS
    opens_seq = position == 0
    closes_seq = position == SEQ_DEVS - 1
    residual = hidden.astype(jnp.float32)
    inv_rms = lax.rsqrt(jnp.mean(residual * residual, axis=1, keepdims=True) + EPSILON)
    normed = residual * inv_rms
    normed_low = (normed * norm_gain).astype(jnp.bfloat16)
    zx_flat = zx_proj.reshape(model_width, 2 * inner_local)
    zx_out = jnp.dot(normed_low, zx_flat, preferred_element_type=jnp.float32)
    gate_low = zx_out[:, :inner_local].astype(jnp.bfloat16)
    bc_out = jnp.dot(normed_low, bc_proj, preferred_element_type=jnp.float32)
    dt_raw = jnp.dot(normed_low, dt_proj, preferred_element_type=jnp.float32)
    conv_in = jnp.concatenate(
        [zx_out[:, inner_local:].astype(jnp.bfloat16), bc_out.astype(jnp.bfloat16)], axis=1
    )
    conv_weights = jnp.concatenate([conv_x, conv_bc], axis=1)
    rim_rows = shifted(conv_in[tokens - (KCONV - 1) :], "dp", 1)
    rim_rows = jnp.where(opens_seq, jnp.zeros_like(rim_rows), rim_rows)
    padded = jnp.concatenate([rim_rows, conv_in], axis=0).astype(jnp.float32)
    conv_pre = conv_weights[KCONV] + conv_weights[0] * padded[0:tokens]
    for tap_index in range(1, KCONV):
        conv_pre = conv_pre + conv_weights[tap_index] * padded[tap_index : tap_index + tokens]
    conv_act = swish_value(conv_pre)
    inputs = conv_act[:, :inner_local].reshape(blocks, BLOCK_LEN, heads_local, head_size)
    b_rows = conv_act[:, inner_local : inner_local + state_size].reshape(
        blocks, BLOCK_LEN, state_size
    )
    c_rows = conv_act[:, inner_local + state_size :].reshape(blocks, BLOCK_LEN, state_size)
    dt_pre = dt_raw + dt_bias
    step_size = jax.nn.softplus(dt_pre)
    decay_rate = -jnp.exp(a_log)
    step_blocks = step_size.reshape(blocks, BLOCK_LEN, heads_local)
    cumulative = jnp.cumsum(
        (decay_rate * step_size).reshape(blocks, BLOCK_LEN, heads_local), axis=1
    )
    cumul_heads = jnp.swapaxes(cumulative, 1, 2)
    step_heads = jnp.swapaxes(step_blocks, 1, 2)
    row_index = lax.broadcasted_iota(jnp.int32, (BLOCK_LEN, BLOCK_LEN), 0)
    col_index = lax.broadcasted_iota(jnp.int32, (BLOCK_LEN, BLOCK_LEN), 1)
    within = (row_index >= col_index)[None, None, :, :]
    spread = cumul_heads[:, :, :, None] - cumul_heads[:, :, None, :]
    decay_pairs = jnp.where(within, jnp.exp(jnp.where(within, spread, 0.0)), 0.0)
    affinity = jnp.einsum("kin,kjn->kij", c_rows, b_rows, precision=PRECISE)
    pair_weight = decay_pairs * step_heads[:, :, None, :]
    mixing = affinity[:, None, :, :] * pair_weight
    intra_out = jnp.einsum("khij,kjhp->kihp", mixing, inputs, precision=PRECISE)
    end_exp = jnp.exp(cumulative[:, -1:, :] - cumulative)
    to_end = end_exp * step_blocks
    sent_state = jnp.einsum("kjhp,kjn->khpn", to_end[..., None] * inputs, b_rows, precision=PRECISE)
    block_decay = jnp.exp(cumulative[:, -1, :])
    zero_state = jnp.zeros((heads_local, head_size, state_size), jnp.float32)
    local_in = [zero_state]
    decay_before = [jnp.ones((heads_local,), jnp.float32)]
    for block_index in range(blocks):
        local_in.append(
            block_decay[block_index][:, None, None] * local_in[-1] + sent_state[block_index]
        )
        decay_before.append(decay_before[-1] * block_decay[block_index])
    own_state = local_in[blocks]
    own_decay = decay_before[blocks]
    arrived = entering(own_state, own_decay, "dp", False)
    states_in = (
        jnp.stack(local_in[:blocks]) + jnp.stack(decay_before[:blocks])[:, :, None, None] * arrived
    )
    exp_cumul = jnp.exp(cumulative)
    inter_out = exp_cumul[..., None] * jnp.einsum(
        "kin,khpn->kihp", c_rows, states_in, precision=PRECISE
    )
    ssd_out = intra_out + inter_out + d_skip[:, None] * inputs
    ssd_flat = ssd_out.reshape(tokens, inner_local)
    gate_wide = gate_low.astype(jnp.float32)
    gate_act = swish_value(gate_wide)
    gated_out = ssd_flat * gate_act
    gated_low = (gated_out * gate_gain).astype(jnp.bfloat16)
    grad_top = cotangent.astype(jnp.float32)
    partial_proj = product_nt(gated_low, out_proj)
    square_sum, grad_inv = lax.psum(
        (jnp.sum(gated_out * gated_out, axis=1), jnp.sum(grad_top * partial_proj, axis=1)),
        "tensor",
    )
    inv_gate = lax.rsqrt(square_sum / inner_total + EPSILON)[:, None]
    parts = lax.axis_size("tensor")
    own_rows = tokens // parts
    first_row = lax.axis_index("tensor") * own_rows

    def rows_of(array):
        return lax.dynamic_slice_in_dim(array, first_row, own_rows, 0)

    def row_sums(partial):
        return lax.psum_scatter(
            partial.astype(jnp.bfloat16), "tensor", scatter_dimension=0, tiled=True
        ).astype(jnp.float32)

    proj_rows = row_sums(partial_proj)
    out_rows = (rows_of(residual) + rows_of(inv_gate) * proj_rows).astype(jnp.bfloat16)
    block_out = lax.all_gather(out_rows, "tensor", axis=0, tiled=True)
    grad_proj = (inv_gate * grad_top).astype(jnp.bfloat16)
    grad_inv = grad_inv[:, None]
    grad_gated_low = jnp.dot(grad_proj, out_proj, preferred_element_type=jnp.float32)
    grad_out_local = product_tn(grad_proj, gated_low)
    grad_gate_gain = jnp.sum(grad_gated_low * gated_out, axis=0)
    grad_gated = (
        grad_gated_low * gate_gain
        - grad_inv * inv_gate * inv_gate * inv_gate / inner_total * gated_out
    )
    grad_ssd = (grad_gated * gate_act).reshape(blocks, BLOCK_LEN, heads_local, head_size)
    grad_gate = (grad_gated * ssd_flat * swish_slope(gate_wide)).astype(jnp.bfloat16)
    grad_skip = jnp.sum(grad_ssd * inputs, axis=(0, 1, 3))
    grad_scaled = grad_ssd * exp_cumul[..., None]
    grad_c = jnp.einsum("kihp,khpn->kin", grad_scaled, states_in, precision=PRECISE)
    grad_from_out = jnp.einsum("kihp,kin->khpn", grad_scaled, c_rows, precision=PRECISE)
    grad_cumul = jnp.sum(grad_ssd * inter_out, axis=3)
    grad_mixing = jnp.einsum("kihp,kjhp->khij", grad_ssd, inputs, precision=PRECISE)
    grad_inputs = d_skip[:, None] * grad_ssd + jnp.einsum(
        "khij,kihp->kjhp", mixing, grad_ssd, precision=PRECISE
    )
    grad_affinity = jnp.sum(grad_mixing * pair_weight, axis=1)
    grad_pairs = grad_mixing * affinity[:, None, :, :] * decay_pairs
    grad_step = jnp.swapaxes(jnp.sum(grad_pairs, axis=2), 1, 2)
    grad_spread = grad_pairs * step_heads[:, :, None, :]
    grad_cumul = grad_cumul + jnp.swapaxes(
        jnp.sum(grad_spread, axis=3) - jnp.sum(grad_spread, axis=2), 1, 2
    )
    grad_c = grad_c + jnp.einsum("kij,kjn->kin", grad_affinity, b_rows, precision=PRECISE)
    grad_b = jnp.einsum("kij,kin->kjn", grad_affinity, c_rows, precision=PRECISE)
    local_grad = [zero_state]
    decay_after = [jnp.ones((heads_local,), jnp.float32)]
    for block_index in reversed(range(blocks)):
        local_grad.insert(
            0, grad_from_out[block_index] + block_decay[block_index][:, None, None] * local_grad[0]
        )
        decay_after.insert(0, decay_after[0] * block_decay[block_index])
    own_grad = local_grad[0]
    back_arrived = entering(own_grad, own_decay, "dp", True)
    grad_states = jnp.stack(local_grad) + jnp.stack(decay_after)[:, :, None, None] * back_arrived
    grad_send = grad_states[1:]
    state_back = jnp.einsum("khpn,kjn->kjhp", grad_send, b_rows, precision=PRECISE)
    grad_to_end = jnp.sum(inputs * state_back, axis=3)
    grad_inputs = grad_inputs + to_end[..., None] * state_back
    grad_b = grad_b + jnp.einsum(
        "kjhp,khpn->kjn", to_end[..., None] * inputs, grad_send, precision=PRECISE
    )
    grad_step = grad_step + grad_to_end * end_exp
    weighted = grad_to_end * to_end
    grad_last = jnp.sum(weighted, axis=1) + block_decay * jnp.sum(
        grad_send * states_in, axis=(2, 3)
    )
    grad_cumul = (grad_cumul - weighted).at[:, -1, :].add(grad_last)
    grad_log = jnp.flip(jnp.cumsum(jnp.flip(grad_cumul, 1), axis=1), 1).reshape(tokens, heads_local)
    grad_a_log = decay_rate * jnp.sum(grad_log * step_size, axis=0)
    grad_dt_pre = (grad_step.reshape(tokens, heads_local) + decay_rate * grad_log) * jax.nn.sigmoid(
        dt_pre
    )
    grad_dt_bias = jnp.sum(grad_dt_pre, axis=0)
    grad_dt_low = grad_dt_pre.astype(jnp.bfloat16)
    grad_bc_act = lax.psum(
        jnp.concatenate([grad_b, grad_c], axis=2).reshape(tokens, 2 * state_size), "tensor"
    )
    grad_act = jnp.concatenate([grad_inputs.reshape(tokens, inner_local), grad_bc_act], axis=1)
    grad_pre = grad_act * swish_slope(conv_pre)
    rim_back = shifted(grad_pre[: KCONV - 1], "dp", -1)
    rim_back = jnp.where(closes_seq, 0.0, rim_back)
    extended = jnp.concatenate([grad_pre, rim_back], axis=0)
    grad_conv_in = conv_weights[0] * extended[KCONV - 1 : KCONV - 1 + tokens]
    for tap_index in range(1, KCONV):
        grad_conv_in = (
            grad_conv_in
            + conv_weights[tap_index]
            * extended[KCONV - 1 - tap_index : KCONV - 1 - tap_index + tokens]
        )
    grad_taps = jnp.stack(
        [
            jnp.sum(grad_pre * padded[tap_index : tap_index + tokens], axis=0)
            for tap_index in range(KCONV)
        ]
        + [jnp.sum(grad_pre, axis=0)]
    )
    grad_inner_low = grad_conv_in[:, :inner_local].astype(jnp.bfloat16)
    grad_bc_low = grad_conv_in[:, inner_local:].astype(jnp.bfloat16)
    grad_zx_low = jnp.concatenate([grad_gate, grad_inner_low], axis=1)
    grad_normed_part = product_nt(grad_zx_low, zx_flat) + product_nt(grad_dt_low, dt_proj)
    grad_normed_part, block_out = lax.optimization_barrier((grad_normed_part, block_out))
    grad_normed = row_sums(grad_normed_part) + product_nt(rows_of(grad_bc_low), bc_proj)
    normed_rows = rows_of(normed)
    grad_norm_local = jnp.sum(grad_normed * normed_rows, axis=0)
    grad_scaled_in = grad_normed * norm_gain
    grad_resid = rows_of(inv_rms) * (
        grad_scaled_in - normed_rows * jnp.mean(grad_scaled_in * normed_rows, axis=1, keepdims=True)
    )
    hidden_rows = (rows_of(grad_top) + grad_resid).astype(jnp.bfloat16)
    grad_hidden = lax.all_gather(hidden_rows, "tensor", axis=0, tiled=True)
    grad_norm_local = lax.psum(grad_norm_local, "tensor")
    low = jnp.bfloat16
    grad_z_local = product_tn(normed_low, grad_gate)
    grad_x_local = product_tn(normed_low, grad_inner_low)
    grad_bc_local = product_tn(normed_low, grad_bc_low)
    grad_dt_local = product_tn(normed_low, grad_dt_low)

    def spread_sum(local):
        return halving_sum(local, "dp")

    grad_out_proj = spread_sum(grad_out_local)
    grad_zx_proj = jnp.stack([spread_sum(grad_z_local), spread_sum(grad_x_local)], axis=1)
    grad_bc_proj = spread_sum(grad_bc_local)
    grad_dt_proj = spread_sum(grad_dt_local)
    (
        grad_norm_gain,
        grad_conv_x,
        grad_conv_bc,
        grad_dt_bias,
        grad_a_log,
        grad_d_skip,
        grad_gate_gain,
    ) = lax.psum(
        (
            grad_norm_local,
            grad_taps[:, :inner_local],
            grad_taps[:, inner_local:],
            grad_dt_bias,
            grad_a_log,
            grad_skip,
            grad_gate_gain,
        ),
        "dp",
    )
    return (
        block_out,
        grad_hidden,
        grad_norm_gain,
        grad_zx_proj,
        grad_bc_proj,
        grad_dt_proj,
        grad_conv_x,
        grad_conv_bc,
        grad_dt_bias,
        grad_a_log,
        grad_d_skip,
        grad_gate_gain,
        grad_out_proj,
    )


def solution(mesh):
    in_specs = (
        P("dp", None),
        P(),
        P(None, None, "tensor"),
        P(),
        P(None, "tensor"),
        P(None, "tensor"),
        P(),
        P("tensor"),
        P("tensor"),
        P("tensor"),
        P("tensor"),
        P(None, "tensor"),
        P("dp", None),
    )
    out_specs = (
        P("dp", None),
        P("dp", None),
        P(),
        P("dp", None, "tensor"),
        P("dp", None),
        P("dp", "tensor"),
        P(None, "tensor"),
        P(),
        P("tensor"),
        P("tensor"),
        P("tensor"),
        P("tensor"),
        P("dp", "tensor"),
    )
    return jax.shard_map(shards, mesh=mesh, in_specs=in_specs, out_specs=out_specs, check_vma=False)
```
